256 devices in a mesh: srv: 8 (over y, core), head: 4 (over x), wsh: 8 (over z).
Axes of the slice: x: 4, y: 4, z: 8, core: 2. Of those that a mesh axis runs over, the one named last changes fastest.
Arguments:
- queries: bfloat16 [12288, 8192], P(('srv', 'wsh'), 'head'), may hold values from -4.5 to 4.5
- keys: bfloat16 [12288, 1024], P(('srv', 'wsh'), 'head'), may hold values from -4.5 to 4.5
- values: bfloat16 [12288, 1024], P(('srv', 'wsh'), 'head'), may hold values from -6 to 6
- doc_ids: int32 [12288], replicated, may hold values from 0 to 2, never falling along the last dimension, each value on 1 to 11904 neighbouring positions
- block_mask: int32 [64, 4], replicated, may hold values from 0 to 1, as said below
- out_weight: bfloat16 [8192, 8192], P(('head', 'wsh')), may hold values from -0.0625 to 0.0625
Outputs:
- projected: bfloat16 [12288, 8192], P(('srv', 'head', 'wsh'))
The draws below stay inside these ranges and needn't reach their ends.
Inputs may be any that keep to these rules, and one draw needn't show every extreme that they name: `block_mask`: column 0 is 1 in every row; other entries are 0 or 1.
All inputs are finite; a program needn't handle non-finite values.
Results may differ from the reference program's by a relative error of at most 0.017.
Values may be sent and summed in bfloat16 or wider, within the bound.
A program may use at most 128 MiB of HBM per device.

```python
import math
import jax
import jax.numpy as jnp
import numpy as np
from jax import lax

QUERY_HEAD_COUNT = 64
KEY_VALUE_HEADS = 8
HEAD_SIZE = 128
D = 8192
SLAB_TOKENS = 192
SLAB_REACH = 4
SLAB_COUNT = 64
PACKED_TOKENS = 12288
ROWS_DEV = 256


def shared_keys(key):
    base = jax.random.fold_in(key, 7211)
    first = jax.random.fold_in(base, 0)
    window_width = KEY_VALUE_HEADS * HEAD_SIZE
    drawn = jnp.clip(jax.random.normal(first, (PACKED_TOKENS, window_width), jnp.float32), -4.5, 4.5)
    return drawn


def draw_keys(key, part):
    drawn = shared_keys(key)
    return drawn.astype(jnp.bfloat16)


def draw_queries(key, part):
    own_key = jax.random.fold_in(key, 5309)
    query_draw = jnp.clip(jax.random.normal(own_key, (PACKED_TOKENS, QUERY_HEAD_COUNT * HEAD_SIZE), jnp.float32), -4.5, 4.5)
    return query_draw.astype(jnp.bfloat16)


def draw_block_mask(key, part):
    levels = jax.random.randint(jax.random.fold_in(key, 31), (SLAB_COUNT, SLAB_REACH), 0, 4)
    opened = jnp.where(levels > 0, 1, 0).astype(jnp.int32)
    return opened.at[:, 0].set(1)


def steps_of(key, dims, pieces, least, top_value):
    gain, own = 1.0, jax.random.fold_in(key, 6)
    for position, parts in pieces:
        draws = jnp.exp(jax.random.uniform(jax.random.fold_in(own, position), (parts,), jnp.float32, least / len(pieces), top_value / len(pieces)))
        gain = gain * jnp.repeat(draws, dims[position] // parts).reshape([-1 if axis == position else 1 for axis in range(len(dims))])
    return gain


def split_up(number_of, total, reach, slope):
    weights = [(1 << 20) // math.isqrt(rank ** slope) + 1 for rank in range(2, number_of + 1)]
    spare, holding = total - reach - (number_of - 1), [1] * (number_of - 1)
    while spare > 0:
        free = [i for i in range(number_of - 1) if holding[i] < reach]
        pool, remaining = sum([weights[i] for i in free]), spare
        for i in free:
            more = min(reach - holding[i], max(1, remaining * weights[i] // pool), spare)
            holding[i] = holding[i] + more
            spare = spare - more
    return np.array([reach] + holding)


def uneven_parts(key, number_of, total, most, slope):
    if number_of == 2:
        one = jax.random.randint(key, (), max(1, total - most), min(most, total - 1) + 1)
        return jnp.stack([one, total - one])
    tallies = jnp.asarray(split_up(number_of, total, most, slope), jnp.int32)
    pairs = (number_of - 1) // 2
    giver, receiver = tallies[1:1 + 2 * pairs:2], tallies[2:2 + 2 * pairs:2]
    margin = jnp.minimum(giver - 1, most - receiver)
    moved = jax.random.randint(jax.random.fold_in(key, 1), (pairs,), 0, 1 << 20) % (margin + 1)
    tallies = tallies.at[1:1 + 2 * pairs:2].set(giver - moved).at[2:2 + 2 * pairs:2].set(receiver + moved)
    return tallies[jax.random.permutation(jax.random.fold_in(key, 2), number_of)]


def noise(key, shape, width, limit, cuts=(), kind=jnp.bfloat16):
    drawn = width * jax.random.normal(key, shape, jnp.float32)
    if cuts:
        drawn = drawn * steps_of(key, shape, cuts, -0.22, 0.18)
    return jnp.clip(drawn, -limit, limit).astype(kind)


def setup_inputs(seed: int = 0) -> dict:
    arg_keys = jax.random.split(jax.random.key(seed), 7)
    queries = draw_queries(jax.random.fold_in(arg_keys[6], 71), 0)
    keys = draw_keys(jax.random.fold_in(arg_keys[6], 71), 0)
    values = noise(arg_keys[2], (PACKED_TOKENS, KEY_VALUE_HEADS * HEAD_SIZE), 1.0, 6.0, ((0, 64), (1, 4)))
    doc_ids = jnp.searchsorted(jnp.cumsum(uneven_parts(arg_keys[3], 3, PACKED_TOKENS, PACKED_TOKENS - 2 * SLAB_TOKENS, 2)), jnp.arange(PACKED_TOKENS), side="right").astype(jnp.int32)
    block_mask = draw_block_mask(jax.random.fold_in(arg_keys[6], 71), 0)
    out_weight = noise(arg_keys[5], (QUERY_HEAD_COUNT * HEAD_SIZE, D), (QUERY_HEAD_COUNT * HEAD_SIZE) ** -0.5, 0.0625, ((0, 32),))
    return {"queries": queries, "keys": keys, "values": values, "doc_ids": doc_ids, "block_mask": block_mask, "out_weight": out_weight}


def reference(queries, keys, values, doc_ids, block_mask, out_weight):
    query_group_width = QUERY_HEAD_COUNT // KEY_VALUE_HEADS
    score_scale = 1.0 / math.sqrt(HEAD_SIZE)
    query_slab_array = queries.reshape(SLAB_COUNT, SLAB_TOKENS, KEY_VALUE_HEADS, query_group_width, HEAD_SIZE)
    key_slab_array = keys.reshape(SLAB_COUNT, SLAB_TOKENS, KEY_VALUE_HEADS, HEAD_SIZE)
    value_slab_array = values.reshape(SLAB_COUNT, SLAB_TOKENS, KEY_VALUE_HEADS, HEAD_SIZE)
    doc_slabs = doc_ids.reshape(SLAB_COUNT, SLAB_TOKENS)
    padded_keys = jnp.concatenate([jnp.zeros((SLAB_REACH - 1, SLAB_TOKENS, KEY_VALUE_HEADS, HEAD_SIZE), jnp.bfloat16), key_slab_array], axis=0)
    padded_values = jnp.concatenate([jnp.zeros((SLAB_REACH - 1, SLAB_TOKENS, KEY_VALUE_HEADS, HEAD_SIZE), jnp.bfloat16), value_slab_array], axis=0)
    doc_padded = jnp.concatenate([jnp.full((SLAB_REACH - 1, SLAB_TOKENS), -1, jnp.int32), doc_slabs.astype(jnp.int32)], axis=0)

    def one_slab(current_slab):
        query_heads = lax.dynamic_index_in_dim(query_slab_array, current_slab, 0, keepdims=False)
        docs_query = lax.dynamic_index_in_dim(doc_slabs, current_slab, 0, keepdims=False)
        window_keys = lax.dynamic_slice_in_dim(padded_keys, current_slab, SLAB_REACH, 0).reshape(SLAB_REACH * SLAB_TOKENS, KEY_VALUE_HEADS, HEAD_SIZE)
        window_values = lax.dynamic_slice_in_dim(padded_values, current_slab, SLAB_REACH, 0).reshape(SLAB_REACH * SLAB_TOKENS, KEY_VALUE_HEADS, HEAD_SIZE)
        docs_key = lax.dynamic_slice_in_dim(doc_padded, current_slab, SLAB_REACH, 0).reshape(SLAB_REACH * SLAB_TOKENS)
        mask_row = lax.dynamic_index_in_dim(block_mask, current_slab, 0, keepdims=False)
        allowed = jnp.repeat(jnp.flip(mask_row) > 0, SLAB_TOKENS)
        query_pos = current_slab * SLAB_TOKENS + jnp.arange(SLAB_TOKENS, dtype=jnp.int32)
        key_pos = (current_slab - (SLAB_REACH - 1)) * SLAB_TOKENS + jnp.arange(SLAB_REACH * SLAB_TOKENS, dtype=jnp.int32)
        visible = (docs_query[:, None] == docs_key[None, :]) & (key_pos[None, :] <= query_pos[:, None])
        visible = visible & (key_pos >= 0)[None, :] & allowed[None, :]
        scores = jnp.einsum('qhgd,khd->hgqk', query_heads.astype(jnp.float32), window_keys.astype(jnp.float32)) * score_scale
        masked = jnp.where(visible, scores, -1e+30)
        largest = lax.optimization_barrier(jnp.max(masked, axis=-1, keepdims=True))
        softmax_terms = jnp.where(visible, jnp.exp(masked - largest), 0.0)
        normalizer = lax.optimization_barrier(jnp.sum(softmax_terms, axis=-1))
        rounded_terms = softmax_terms.astype(jnp.bfloat16)
        weighted = jnp.einsum('hgqk,khd->qhgd', rounded_terms.astype(jnp.float32), window_values.astype(jnp.float32))
        result = weighted / jnp.transpose(normalizer, (2, 0, 1))[..., None]
        return result.reshape(SLAB_TOKENS, QUERY_HEAD_COUNT * HEAD_SIZE).astype(jnp.bfloat16)
    attention = lax.map(one_slab, jnp.arange(SLAB_COUNT, dtype=jnp.int32)).reshape(PACKED_TOKENS, QUERY_HEAD_COUNT * HEAD_SIZE)
    block_count = QUERY_HEAD_COUNT * HEAD_SIZE // ROWS_DEV

    def add_block(block_index, running):
        lower = (block_index * ROWS_DEV).astype(jnp.int32)
        rows_attention = lax.dynamic_slice_in_dim(attention, lower, ROWS_DEV, 1)
        rows_weight = lax.dynamic_slice_in_dim(out_weight, lower, ROWS_DEV, 0)
        block_term = jnp.dot(rows_attention, rows_weight, preferred_element_type=jnp.float32).astype(jnp.bfloat16)
        block_term = lax.optimization_barrier(block_term)
        return running + block_term.astype(jnp.float32)
    summed = lax.fori_loop(0, block_count, add_block, jnp.zeros((PACKED_TOKENS, D), jnp.float32))
    return summed.astype(jnp.bfloat16)
```

```python
from functools import partial
import math

import jax
import jax.numpy as jnp
from jax import lax
from jax.sharding import PartitionSpec as P

QUERY_HEAD_COUNT = 64
KEY_VALUE_HEADS = 8
HEAD_SIZE = 128
SLAB_REACH = 4


floor_score = -1e30


def shifted(block, axis, distance):
    devices = range(lax.axis_size(axis))
    route = [(i - distance, i) for i in devices if i - distance in devices]
    return lax.ppermute(block, axis, route)


def tile_update(carried, query_heads, key_block, value_block, docs_query, docs_key, causal):
    running_max, running_sum, weighted = carried
    row_count = query_heads.shape[0]
    key_heads = key_block.reshape(row_count, -1, HEAD_SIZE)
    value_heads = value_block.reshape(row_count, -1, HEAD_SIZE)
    scores = jnp.einsum(
        "qhgd,khd->hgqk", query_heads, key_heads, preferred_element_type=jnp.float32
    ) * (1.0 / math.sqrt(HEAD_SIZE))
    visible = docs_query[:, None] == docs_key[None, :]
    if causal:
        query_pos = lax.broadcasted_iota(jnp.int32, (row_count, row_count), 0)
        key_pos = lax.broadcasted_iota(jnp.int32, (row_count, row_count), 1)
        visible = visible & (key_pos <= query_pos)
    masked = jnp.where(visible, scores, floor_score)
    freshest = jnp.maximum(running_max, jnp.max(masked, axis=-1))
    softmax_terms = jnp.where(visible, jnp.exp(masked - freshest[..., None]), 0.0)
    rescale = jnp.exp(running_max - freshest)
    running_sum = running_sum * rescale + jnp.sum(softmax_terms, axis=-1)
    update = jnp.einsum(
        "hgqk,khd->qhgd",
        softmax_terms.astype(jnp.bfloat16),
        value_heads,
        preferred_element_type=jnp.float32,
    )
    weighted = weighted * jnp.transpose(rescale, (2, 0, 1))[..., None] + update
    return (freshest, running_sum, weighted)


def on_device(queries, keys, values, doc_ids, block_mask, out_weight):
    row_count = queries.shape[0]
    kv_local = keys.shape[1] // HEAD_SIZE
    query_group_width = QUERY_HEAD_COUNT // KEY_VALUE_HEADS
    query_heads = queries.reshape(row_count, kv_local, query_group_width, HEAD_SIZE)
    current_slab = lax.axis_index(("srv", "wsh"))
    docs_query = lax.dynamic_slice_in_dim(doc_ids, current_slab * row_count, row_count)
    mask_row = lax.dynamic_index_in_dim(block_mask, current_slab, 0, keepdims=False)
    carried = (
        jnp.full((kv_local, query_group_width, row_count), floor_score, jnp.float32),
        jnp.zeros((kv_local, query_group_width, row_count), jnp.float32),
        jnp.zeros((row_count, kv_local, query_group_width, HEAD_SIZE), jnp.float32),
    )
    for offset in range(SLAB_REACH):
        if offset == 0:
            key_block, value_block = (keys, values)
        else:
            key_block, value_block = shifted((keys, values), ("srv", "wsh"), offset)
        source = current_slab - offset
        docs_key = lax.dynamic_slice_in_dim(doc_ids, jnp.maximum(source, 0) * row_count, row_count)
        live = (mask_row[offset] > 0) & (source >= 0)
        update_tile = partial(
            tile_update,
            query_heads=query_heads,
            key_block=key_block,
            value_block=value_block,
            docs_query=docs_query,
            docs_key=docs_key,
            causal=offset == 0,
        )
        carried = lax.cond(live, update_tile, lambda running: running, carried)
    running_max, running_sum, weighted = carried
    normalizer = jnp.transpose(running_sum, (2, 0, 1))[..., None]
    attention = (weighted / normalizer).reshape(row_count, -1).astype(jnp.bfloat16)
    weight_block = lax.all_to_all(out_weight, "wsh", split_axis=1, concat_axis=0, tiled=True)
    gathered = lax.all_gather(attention, "wsh", axis=0, tiled=True)
    partial_sum = jnp.dot(gathered, weight_block, preferred_element_type=jnp.float32).astype(jnp.bfloat16)
    summed = lax.psum_scatter(partial_sum, "head", scatter_dimension=0, tiled=True)
    return lax.all_to_all(summed, "wsh", split_axis=0, concat_axis=1, tiled=True)


def solution(mesh):
    in_specs = (
        P(("srv", "wsh"), "head"),
        P(("srv", "wsh"), "head"),
        P(("srv", "wsh"), "head"),
        P(),
        P(),
        P(("head", "wsh"), None),
    )
    out_specs = P(("srv", "head", "wsh"), None)
    return jax.shard_map(
        on_device, mesh=mesh, in_specs=in_specs, out_specs=out_specs, check_vma=False
    )
```

```python
from functools import partial
import math

import jax
import jax.numpy as jnp
from jax import lax
from jax.experimental import pallas as pl
from jax.experimental.pallas import tpu as pltpu
from jax.sharding import PartitionSpec as P

HEAD_SIZE = 128
SLAB_REACH = 4
MESH = pl.DeviceIdType.MESH

floor_score = -1e30

ROWS = 192
PIECE = 48
KV = 256
HEADS = 16
KBLK = 2048
NBLK = 2048
NQ = 512
CHUNKS = NBLK // NQ
WIN = SLAB_REACH * ROWS


def mod(a, n):
    return lax.rem(a + n, n)


def aligned(i, step):
    return pl.ds(pl.multiple_of(i * step, step), step)


def kernel(
    q_hbm, k_hbm, v_hbm, bias_hbm, w_hbm, out_hbm,
    q, kw, vw, bias, w, a, abuf, cpart, s1, s2, r1, r2, fb,
    load_sem, h_send, h_recv, wm_send, wm_recv, wp_send, wp_recv, wc_send, wc_recv,
    p_send, p_recv, g_send, g_recv, y_send, y_recv, r1_send, r1_recv, r2_send, r2_recv,
    f_send, f_recv, f_local,
):
    srv = lax.axis_index("srv")
    x = lax.axis_index("head")
    z = lax.axis_index("wsh")
    y = lax.div(srv, 2)
    core = lax.rem(srv, 2)
    slab = srv * 8 + z
    ahead, behind = lax.rem(slab + 1, 64), lax.rem(slab + 63, 64)

    def slab_id(s):
        return {"srv": lax.div(s, 8), "wsh": lax.rem(s, 8)}

    def y_id(step):
        return {"srv": lax.rem(y + step, 4) * 2 + core}

    partner = {"srv": y * 2 + 1 - core}

    def x_id(step):
        return {"head": lax.rem(x + step, 4)}

    def z_id(step):
        return {"wsh": lax.rem(z + step, 8)}

    barrier = pltpu.get_barrier_semaphore()
    greeted = [slab_id(ahead), slab_id(behind), partner, x_id(1), x_id(3)]
    greeted += [y_id(step) for step in (1, 2, 3)] + [z_id(step) for step in range(1, 8)]
    for other in greeted:
        pl.semaphore_signal(barrier, inc=1, device_id=other, device_id_type=MESH)
    pl.semaphore_wait(barrier, len(greeted))

    sent = []

    def remote(src, dst, send_sem, recv_sem, device):
        return pltpu.make_async_remote_copy(
            src_ref=src, dst_ref=dst, send_sem=send_sem, recv_sem=recv_sem,
            device_id=device, device_id_type=MESH,
        )

    def send(*args):
        copy = remote(*args)
        copy.start()
        sent.append(copy)

    def halo(step, which):
        own = (k_hbm, v_hbm)[which]
        window = (kw, vw)[which]
        src = own if step == 1 else window.at[pl.ds((step - 1) * ROWS, ROWS)]
        return remote(
            src, window.at[pl.ds(step * ROWS, ROWS)],
            h_send.at[step - 1, which], h_recv.at[step - 1, which], slab_id(ahead),
        )

    def halo_send(step):
        for which in (0, 1):
            if step > 1:
                halo(step - 1, which).wait_recv()
            copy = halo(step, which)
            copy.start()
            sent.append(copy)

    def w_piece(origin, n):
        return w.at[aligned(core * 8 + origin, 128), pl.ds(n * NQ, NQ)]

    def w_msg(down, n, step):
        sems = (wm_send, wm_recv) if down else (wp_send, wp_recv)
        origin = lax.rem(z + (step - 1 if down else 9 - step), 8)
        if step == 1:
            column = pl.multiple_of(y * NBLK + n * NQ, NQ)
            src = w_hbm.at[aligned(core, 128), pl.ds(column, NQ)]
        else:
            src = w_piece(origin, n)
        return remote(
            src, w_piece(origin, n), sems[0].at[n, step - 1], sems[1].at[n, step - 1],
            z_id(7 if down else 1),
        )

    def w_send(down, n, step):
        copy = w_msg(down, n, step)
        copy.start()
        sent.append(copy)

    def w_wait(down, n, step):
        origin = lax.rem(z + (step if down else 8 - step), 8)
        sems = (wm_send, wm_recv) if down else (wp_send, wp_recv)
        remote(
            w_piece(origin, n), w_piece(origin, n), sems[0].at[n, step - 1],
            sems[1].at[n, step - 1], z_id(7 if down else 1),
        ).wait_recv()

    def fm(n, step):
        w_wait(True, n, step)
        if step < 4:
            w_send(True, n, step + 1)

    def fp(n, step):
        w_wait(False, n, step)
        if step < 3:
            w_send(False, n, step + 1)

    def w_cross(n, half):
        block = w.at[aligned(half, 1024), pl.ds(n * NQ, NQ)]
        return remote(block, block, wc_send.at[n], wc_recv.at[n], partner)

    def w_cross_send(n):
        copy = w_cross(n, core)
        copy.start()
        sent.append(copy)

    halo_send(1)
    loads = [
        pltpu.make_async_copy(q_hbm, q, load_sem.at[0]),
        pltpu.make_async_copy(k_hbm, kw.at[pl.ds(0, ROWS)], load_sem.at[1]),
        pltpu.make_async_copy(v_hbm, vw.at[pl.ds(0, ROWS)], load_sem.at[2]),
        pltpu.make_async_copy(bias_hbm, bias, load_sem.at[3]),
        pltpu.make_async_copy(
            w_hbm.at[aligned(core, 128), aligned(y, NBLK)],
            w.at[aligned(core * 8 + z, 128)], load_sem.at[4],
        ),
    ]
    w_send(True, 0, 1)
    w_send(True, 1, 1)
    for load in loads:
        load.start()
    halo_send(2)
    fm(0, 1)
    fm(1, 1)
    halo_send(3)
    w_send(False, 0, 1)
    w_send(False, 1, 1)
    for load in loads:
        load.wait()
    fm(0, 2)
    fm(1, 2)
    halo(3, 0).wait_recv()
    halo(3, 1).wait_recv()

    factor = math.log2(math.e) / math.sqrt(HEAD_SIZE)

    def a_rows(x_dest, y_src):
        return a.at[aligned(x_dest * 4 + y_src, PIECE)]

    def attend(j):
        rows = aligned(j, PIECE)

        def group(g, carry):
            columns = pl.multiple_of(g * HEAD_SIZE, HEAD_SIZE)
            key = kw[:, pl.ds(columns, HEAD_SIZE)]
            value = vw[:, pl.ds(columns, HEAD_SIZE)]
            stacked = jnp.concatenate(
                [
                    q[rows, pl.ds(pl.multiple_of((g * 8 + i) * HEAD_SIZE, HEAD_SIZE), HEAD_SIZE)]
                    for i in range(8)
                ],
                axis=0,
            )
            scores = lax.dot_general(
                stacked, key, (((1,), (1,)), ((), ())), preferred_element_type=jnp.float32
            )
            scores = scores.reshape(8, PIECE, WIN) * factor + bias[rows, :][None]
            terms = jnp.exp2(scores - jnp.max(scores, axis=-1, keepdims=True))
            total = jnp.sum(terms, axis=-1, keepdims=True)
            weighted = jnp.dot(
                terms.astype(jnp.bfloat16).reshape(8 * PIECE, WIN), value,
                preferred_element_type=jnp.float32,
            ).reshape(8, PIECE, HEAD_SIZE)
            result = (weighted / total).astype(jnp.bfloat16)
            for i in range(8):
                place = pl.multiple_of(((i % 2) * 8 + g * 4 + i // 2) * HEAD_SIZE, HEAD_SIZE)
                abuf[rows, pl.ds(place, HEAD_SIZE)] = result[i]
            return carry

        lax.fori_loop(0, 2, group, 0)

    def p_copy(jj, j, dest):
        return remote(
            abuf.at[aligned(j, PIECE)], a_rows(lax.div(z, 2), y),
            p_send.at[jj], p_recv.at[lax.div(z, 2)], {"wsh": dest},
        )

    def p_place(jj):
        j = lax.rem(jj + lax.div(z, 2), 4)
        return j, 4 * lax.rem(z, 2) + j

    def p_start(jj):
        j, dest = p_place(jj)

        @pl.when(dest == z)
        def _():
            pltpu.make_async_copy(
                abuf.at[aligned(j, PIECE)], a_rows(lax.div(z, 2), y), p_recv.at[lax.div(z, 2)]
            ).start()

        @pl.when(dest != z)
        def _():
            p_copy(jj, j, dest).start()

    def p_piece(jj):
        return lax.rem(lax.rem(z, 4) + 4 - jj, 4)

    def p_wait(jj):
        place = a_rows(p_piece(jj), y)
        pltpu.make_async_copy(place, place, p_recv.at[p_piece(jj)]).wait()

    def g_msg(up, jj, y_src):
        place = a_rows(p_piece(jj), y_src)
        d = 0 if up else 1
        return remote(place, place, g_send.at[d, jj], g_recv.at[d, jj], y_id(1 if up else 3))

    def g_start(jj):
        for up in (True, False):
            copy = g_msg(up, jj, y)
            copy.start()
            sent.append(copy)

    def g_wait(up, jj):
        g_msg(up, jj, lax.rem(y + (3 if up else 1), 4)).wait_recv()

    def y_msg(up, jj, y_src):
        place = a_rows(p_piece(jj), y_src)
        return remote(place, place, y_send.at[jj], y_recv.at[jj], y_id(1 if up else 3))

    def y_relay(jj):
        up = jj < 2
        copy = y_msg(up, jj, lax.rem(y + (3 if up else 1), 4))
        copy.start()
        sent.append(copy)

    def y_wait(jj):
        y_msg(jj < 2, jj, lax.rem(y + 2, 4)).wait_recv()

    fp(0, 1)
    for jj in range(4):
        attend(p_place(jj)[0])
        p_start(jj)
        if jj == 0:
            fp(1, 1)
            fm(0, 3)
        if jj == 1:
            fm(1, 3)
            w_send(True, 2, 1)
            w_send(True, 3, 1)
            fp(0, 2)
        if jj == 2:
            fp(1, 2)
            w_send(False, 2, 1)
            w_send(False, 3, 1)
            p_wait(0)
            g_start(0)
            fm(0, 4)
    fm(1, 4)
    p_wait(1)
    g_start(1)
    fp(0, 3)
    w_cross_send(0)
    fp(1, 3)
    w_cross_send(1)
    p_wait(2)
    g_start(2)
    g_wait(True, 0)
    y_relay(0)
    fm(2, 1)
    fm(3, 1)
    p_wait(3)
    g_start(3)
    g_wait(True, 1)
    y_relay(1)
    fp(2, 1)
    fp(3, 1)
    fm(2, 2)
    fm(3, 2)
    g_wait(False, 2)
    y_relay(2)
    g_wait(False, 3)
    y_relay(3)
    fp(2, 2)
    fp(3, 2)
    fm(2, 3)
    fm(3, 3)
    g_wait(False, 0)
    g_wait(False, 1)
    g_wait(True, 2)
    g_wait(True, 3)
    for jj in range(4):
        y_wait(jj)

    def project(n, step):
        rows = a[aligned(lax.rem(x + step, 4), ROWS), :]
        return jnp.dot(rows, w[:, pl.ds(n * NQ, NQ)], preferred_element_type=jnp.float32)

    half = ROWS // 2

    def r1_msg(up, n):
        d = 0 if up else 1
        return remote(
            s1.at[n, pl.ds(d * half, half)], r1.at[n, d],
            r1_send.at[n, d], r1_recv.at[n, d], x_id(1 if up else 3),
        )

    def r2_msg(up, n):
        d = 0 if up else 1
        return remote(
            s2.at[n, d], r2.at[n, d], r2_send.at[n, d], r2_recv.at[n, d], x_id(1 if up else 3)
        )

    def start(copy):
        copy.start()
        sent.append(copy)

    def stage1(n):
        w_cross(n, 1 - core).wait_recv()
        s1[n] = project(n, 2).astype(jnp.bfloat16)
        start(r1_msg(True, n))
        start(r1_msg(False, n))
        for d, step in ((0, 1), (1, 3), (2, 0)):
            cpart[n, d] = project(n, step)

    def stage2(n):
        for d, up in ((0, True), (1, False)):
            r1_msg(up, n).wait_recv()
            part = pl.ds(d * half, half)
            other = pl.ds((1 - d) * half, half)
            s2[n, d, part, :] = (cpart[n, d, part, :] + r1[n, d].astype(jnp.float32)).astype(jnp.bfloat16)
            s2[n, d, other, :] = cpart[n, d, other, :].astype(jnp.bfloat16)
            start(r2_msg(up, n))

    def f_place(n):
        return out_hbm.at[:, pl.ds(pl.multiple_of(y * NBLK + n * NQ, NQ), NQ)]

    def f_msg(n, step):
        return remote(
            fb.at[n, aligned(lax.rem(y + step, 4), PIECE)], f_place(n),
            f_send.at[n, step - 1], f_recv.at[n, step - 1], y_id(step),
        )

    def f_own(n):
        return pltpu.make_async_copy(fb.at[n, aligned(y, PIECE)], f_place(n), f_local.at[n])

    def stage3(n):
        r2_msg(True, n).wait_recv()
        r2_msg(False, n).wait_recv()
        total = cpart[n, 2] + r2[n, 0].astype(jnp.float32) + r2[n, 1].astype(jnp.float32)
        fb[n] = total.astype(jnp.bfloat16)
        for step in (1, 2, 3):
            start(f_msg(n, step))
        f_own(n).start()

    stage1(0)
    stage1(1)
    stage2(0)
    fm(2, 4)
    fm(3, 4)
    fp(2, 3)
    w_cross_send(2)
    fp(3, 3)
    w_cross_send(3)
    stage2(1)
    stage3(0)
    stage1(2)
    stage3(1)
    stage1(3)
    stage2(2)
    stage2(3)
    stage3(2)
    stage3(3)

    for n in range(CHUNKS):
        f_own(n).wait()
        for step in (1, 2, 3):
            source = lax.rem(y + 4 - step, 4)
            place = out_hbm.at[:, pl.ds(pl.multiple_of(source * NBLK + n * NQ, NQ), NQ)]
            remote(
                fb.at[n, aligned(y, PIECE)], place,
                f_send.at[n, step - 1], f_recv.at[n, step - 1], y_id(step),
            ).wait_recv()
    for copy in sent:
        copy.wait_send()
    for jj in range(4):
        j, dest = p_place(jj)

        @pl.when(dest != z)
        def _():
            p_copy(jj, j, dest).wait_send()


def on_device(queries, keys, values, doc_ids, block_mask, out_weight):
    slab = lax.axis_index(("srv", "wsh"))
    docs_query = lax.dynamic_slice_in_dim(doc_ids, slab * ROWS, ROWS)
    mask_row = lax.dynamic_index_in_dim(block_mask, slab, 0, keepdims=False)
    parts = []
    for offset in range(SLAB_REACH):
        source = slab - offset
        docs_key = lax.dynamic_slice_in_dim(doc_ids, jnp.maximum(source, 0) * ROWS, ROWS)
        seen = docs_query[:, None] == docs_key[None, :]
        if offset == 0:
            query_pos = lax.broadcasted_iota(jnp.int32, (ROWS, ROWS), 0)
            key_pos = lax.broadcasted_iota(jnp.int32, (ROWS, ROWS), 1)
            seen = seen & (key_pos <= query_pos)
        parts.append(seen & (mask_row[offset] > 0) & (source >= 0))
    bias = jnp.where(jnp.concatenate(parts, axis=1), 0.0, floor_score).astype(jnp.float32)

    any_space = pl.BlockSpec(memory_space=pl.ANY)
    dma = pltpu.SemaphoreType.DMA
    bf16, f32 = jnp.bfloat16, jnp.float32
    return pl.pallas_call(
        kernel,
        out_shape=jax.ShapeDtypeStruct((PIECE, 4 * NBLK), bf16),
        in_specs=[any_space] * 5,
        out_specs=any_space,
        scratch_shapes=[
            pltpu.VMEM((ROWS, KBLK), bf16),
            pltpu.VMEM((WIN, KV), bf16),
            pltpu.VMEM((WIN, KV), bf16),
            pltpu.VMEM((ROWS, WIN), f32),
            pltpu.VMEM((KBLK, NBLK), bf16),
            pltpu.VMEM((4 * ROWS, KBLK), bf16),
            pltpu.VMEM((ROWS, KBLK), bf16),
            pltpu.VMEM((CHUNKS, 3, ROWS, NQ), f32),
            pltpu.VMEM((CHUNKS, ROWS, NQ), bf16),
            pltpu.VMEM((CHUNKS, 2, ROWS, NQ), bf16),
            pltpu.VMEM((CHUNKS, 2, ROWS // 2, NQ), bf16),
            pltpu.VMEM((CHUNKS, 2, ROWS, NQ), bf16),
            pltpu.VMEM((CHUNKS, ROWS, NQ), bf16),
            dma((5,)),
            dma((3, 2)), dma((3, 2)),
            dma((CHUNKS, 4)), dma((CHUNKS, 4)),
            dma((CHUNKS, 3)), dma((CHUNKS, 3)),
            dma((CHUNKS,)), dma((CHUNKS,)),
            dma((4,)), dma((4,)),
            dma((2, 4)), dma((2, 4)),
            dma((4,)), dma((4,)),
            dma((CHUNKS, 2)), dma((CHUNKS, 2)),
            dma((CHUNKS, 2)), dma((CHUNKS, 2)),
            dma((CHUNKS, 3)), dma((CHUNKS, 3)), dma((CHUNKS,)),
        ],
        compiler_params=pltpu.CompilerParams(
            collective_id=0, has_side_effects=True, vmem_limit_bytes=60 * 1024 * 1024
        ),
    )(queries, keys, values, bias, out_weight)


def solution(mesh):
    in_specs = (
        P(("srv", "wsh"), "head"),
        P(("srv", "wsh"), "head"),
        P(("srv", "wsh"), "head"),
        P(),
        P(),
        P(("head", "wsh"), None),
    )
    out_specs = P(("srv", "head", "wsh"), None)
    return jax.shard_map(
        on_device, mesh=mesh, in_specs=in_specs, out_specs=out_specs, check_vma=False
    )
```

```python
from functools import partial
import math

import jax
import jax.numpy as jnp
from jax import lax
from jax.experimental import pallas as pl
from jax.experimental.pallas import tpu as pltpu
from jax.sharding import PartitionSpec as P

HEAD_SIZE = 128
SLAB_REACH = 4
MESH = pl.DeviceIdType.MESH

floor_score = -1e30

ROWS = 192
PIECE = 48
KV = 256
HEADS = 16
KBLK = 2048
NBLK = 2048
NQ = 512
CHUNKS = NBLK // NQ
WIN = SLAB_REACH * ROWS
PAIR = 2 * ROWS
PARTS = 3
SUB = PIECE // PARTS


def mod(a, n):
    return lax.rem(a + n, n)


def aligned(i, step):
    return pl.ds(pl.multiple_of(i * step, step), step)


def kernel(
    q_hbm, k_hbm, v_hbm, docs, mask, w_hbm, out_hbm,
    q, kw, vw, bias, peak, acc, w, a, abuf, cpart, s1, s2, r1, r2, fb,
    load_sem, h_send, h_recv, wm_send, wm_recv, wp_send, wp_recv, wc_send, wc_recv,
    p_send, p_recv, g_send, g_recv, y_send, y_recv, r1_send, r1_recv, r2_send, r2_recv,
    f_send, f_recv, f_local,
):
    srv = lax.axis_index("srv")
    x = lax.axis_index("head")
    z = lax.axis_index("wsh")
    y = lax.div(srv, 2)
    core = lax.rem(srv, 2)
    slab = srv * 8 + z
    ahead, behind = lax.rem(slab + 1, 64), lax.rem(slab + 63, 64)

    def slab_id(s):
        return {"srv": lax.div(s, 8), "wsh": lax.rem(s, 8)}

    def y_id(step):
        return {"srv": lax.rem(y + step, 4) * 2 + core}

    partner = {"srv": y * 2 + 1 - core}

    def x_id(step):
        return {"head": lax.rem(x + step, 4)}

    def z_id(step):
        return {"wsh": lax.rem(z + step, 8)}

    barrier = pltpu.get_barrier_semaphore()
    greeted = [slab_id(ahead), slab_id(behind), partner, x_id(1), x_id(3)]
    greeted += [y_id(step) for step in (1, 2, 3)] + [z_id(step) for step in range(1, 8)]
    for other in greeted:
        pl.semaphore_signal(barrier, inc=1, device_id=other, device_id_type=MESH)
    loads = [
        pltpu.make_async_copy(q_hbm, q, load_sem.at[0]),
        pltpu.make_async_copy(k_hbm, kw.at[pl.ds(0, ROWS)], load_sem.at[1]),
        pltpu.make_async_copy(v_hbm, vw.at[pl.ds(0, ROWS)], load_sem.at[2]),
    ]
    for part in (0, 1):
        loads.append(
            pltpu.make_async_copy(
                w_hbm.at[pl.ds(part * 128, 128), aligned(y, NBLK)],
                w.at[aligned(part * 8 + z, 128)], load_sem.at[3 + part],
            )
        )
    for load in loads:
        load.start()

    def docs_of(source):
        first = lax.div(source * 3, 2)
        row, after = docs[pl.ds(first, 1), :], docs[pl.ds(first + 1, 1), :]
        even = jnp.concatenate([row, after[:, :64]], axis=1)
        odd = jnp.concatenate([row[:, 64:], after], axis=1)
        return jnp.where(lax.rem(source, 2) == 0, even, odd).astype(jnp.float32)

    row_ids = lax.broadcasted_iota(jnp.int32, (ROWS, ROWS), 0)
    column_ids = lax.broadcasted_iota(jnp.int32, (ROWS, ROWS), 1)
    docs_query = jnp.sum(
        jnp.where(row_ids == column_ids, docs_of(slab), 0.0), axis=1, keepdims=True
    )
    for offset in range(SLAB_REACH):
        source = slab - offset
        live = (mask[offset, slab] > 0) & (source >= 0)
        seen = docs_query == docs_of(jnp.maximum(source, 0))
        if offset == 0:
            seen = seen & (column_ids <= row_ids)
        bias[:, pl.ds(offset * ROWS, ROWS)] = jnp.where(
            seen, jnp.where(live, 0.0, floor_score), floor_score
        )
    pl.semaphore_wait(barrier, len(greeted))

    sent = []

    def remote(src, dst, send_sem, recv_sem, device):
        return pltpu.make_async_remote_copy(
            src_ref=src, dst_ref=dst, send_sem=send_sem, recv_sem=recv_sem,
            device_id=device, device_id_type=MESH,
        )

    def halo(step, which):
        own = (k_hbm, v_hbm)[which]
        window = (kw, vw)[which]
        src = own if step == 1 else window.at[pl.ds((step - 1) * ROWS, ROWS)]
        return remote(
            src, window.at[pl.ds(step * ROWS, ROWS)],
            h_send.at[step - 1, which], h_recv.at[step - 1, which], slab_id(ahead),
        )

    def halo_send(step):
        for which in (0, 1):
            if step > 1:
                halo(step - 1, which).wait_recv()
            copy = halo(step, which)
            copy.start()
            sent.append(copy)

    def halo_wait():
        halo(3, 0).wait_recv()
        halo(3, 1).wait_recv()

    def w_piece(origin, n):
        return w.at[aligned(core * 8 + origin, 128), pl.ds(n * NQ, NQ)]

    def w_msg(down, n, step):
        sems = (wm_send, wm_recv) if down else (wp_send, wp_recv)
        origin = lax.rem(z + (step - 1 if down else 9 - step), 8)
        if step == 1:
            column = pl.multiple_of(y * NBLK + n * NQ, NQ)
            src = w_hbm.at[aligned(core, 128), pl.ds(column, NQ)]
        else:
            src = w_piece(origin, n)
        return remote(
            src, w_piece(origin, n), sems[0].at[n, step - 1], sems[1].at[n, step - 1],
            z_id(7 if down else 1),
        )

    def w_send(down, n, step):
        copy = w_msg(down, n, step)
        copy.start()
        sent.append(copy)

    def w_wait(down, n, step):
        origin = lax.rem(z + (step if down else 8 - step), 8)
        sems = (wm_send, wm_recv) if down else (wp_send, wp_recv)
        remote(
            w_piece(origin, n), w_piece(origin, n), sems[0].at[n, step - 1],
            sems[1].at[n, step - 1], z_id(7 if down else 1),
        ).wait_recv()

    def w_cross(down, n, step, half):
        origin = lax.rem(z + (step if down else 8 - step), 8)
        block = w.at[aligned(half * 8 + origin, 128), pl.ds(n * NQ, NQ)]
        index = step - 1 if down else step + 3
        return remote(block, block, wc_send.at[n, index], wc_recv.at[n, index], partner)

    def arrive(down, n, step):
        w_wait(down, n, step)
        if step < (4 if down else 3):
            w_send(down, n, step + 1)
        copy = w_cross(down, n, step, core)
        copy.start()
        sent.append(copy)

    def w_complete(n):
        for step in (1, 2, 3, 4):
            w_cross(True, n, step, 1 - core).wait_recv()
        for step in (1, 2, 3):
            w_cross(False, n, step, 1 - core).wait_recv()

    D, U = True, False

    factor = math.log2(math.e) / math.sqrt(HEAD_SIZE)

    def attend(late, part, g):
        place = part * 2 + g
        columns = aligned(g, HEAD_SIZE)
        keys_seen = pl.ds(late * PAIR, PAIR)
        key, value = kw[keys_seen, columns], vw[keys_seen, columns]
        rows = [aligned(j * PARTS + part, SUB) for j in range(4)]
        stacked = jnp.concatenate(
            [q[rows[j], aligned(g * 8 + i, HEAD_SIZE)] for j in range(4) for i in range(8)], axis=0
        )
        scores = lax.dot_general(
            stacked, key, (((1,), (1,)), ((), ())), preferred_element_type=jnp.float32
        )
        scores = jnp.concatenate(
            [
                scores[j * 8 * SUB : (j + 1) * 8 * SUB].reshape(8, SUB, PAIR) * factor
                + bias[rows[j], keys_seen][None]
                for j in range(4)
            ],
            axis=0,
        ).reshape(32 * SUB, PAIR)
        largest = jnp.broadcast_to(jnp.max(scores, axis=-1, keepdims=True), (32 * SUB, HEAD_SIZE))
        if late:
            before = peak[place]
            largest = jnp.maximum(largest, before)
        terms = jnp.exp2(scores - jnp.concatenate([largest] * 3, axis=1)).astype(jnp.bfloat16)
        widened = jnp.concatenate([value, jnp.ones_like(value)], axis=1)
        both = jnp.dot(terms, widened, preferred_element_type=jnp.float32)
        if not late:
            peak[place] = largest
            acc[place] = both
            return
        rescale = jnp.exp2(before - largest)
        both = both + acc[place] * jnp.concatenate([rescale] * 2, axis=1)
        result = (both[:, :HEAD_SIZE] / both[:, HEAD_SIZE:]).astype(jnp.bfloat16)
        for j in range(4):
            for i in range(8):
                abuf[
                    aligned(part * 4 + j, SUB), aligned((i % 2) * 8 + g * 4 + i // 2, HEAD_SIZE)
                ] = result[(j * 8 + i) * SUB : (j * 8 + i + 1) * SUB]

    def attend_early():
        def step(i, carry):
            attend(0, lax.div(i, 2), lax.rem(i, 2))
            return carry

        lax.fori_loop(0, 2 * PARTS, step, 0)

    def attend_late(part):
        def step(g, carry):
            attend(1, part, g)
            return carry

        lax.fori_loop(0, 2, step, 0)

    def p_place(part, x_dest):
        return a.at[aligned((part * 4 + y) * 4 + x_dest, SUB)]

    def p_route(jj):
        j = lax.rem(jj + lax.div(z, 2), 4)
        return j, 4 * lax.rem(z, 2) + j

    def p_copy(part, jj):
        j, dest = p_route(jj)
        return remote(
            abuf.at[aligned(part * 4 + j, SUB)], p_place(part, lax.div(z, 2)),
            p_send.at[part, jj], p_recv.at[part, lax.div(z, 2)], {"wsh": dest},
        )

    def p_start(part):
        for jj in range(4):
            j, dest = p_route(jj)

            @pl.when(dest == z)
            def _():
                pltpu.make_async_copy(
                    abuf.at[aligned(part * 4 + j, SUB)], p_place(part, lax.div(z, 2)),
                    p_recv.at[part, lax.div(z, 2)],
                ).start()

            @pl.when(dest != z)
            def _():
                p_copy(part, jj).start()

    def p_wait(part):
        for x_dest in range(4):
            place = p_place(part, x_dest)
            pltpu.make_async_copy(place, place, p_recv.at[part, x_dest]).wait()

    def start(copy):
        copy.start()
        sent.append(copy)

    def g_msg(d, part, y_src):
        place = a.at[aligned(part * 4 + y_src, 4 * SUB)]
        return remote(place, place, g_send.at[d, part], g_recv.at[d, part], y_id((1, 3)[d]))

    def g_start(part):
        for d in (0, 1):
            start(g_msg(d, part, y))

    def y_msg(d, part, y_src):
        place = a.at[aligned((part * 4 + y_src) * 2 + d, 2 * SUB)]
        return remote(place, place, y_send.at[d, part], y_recv.at[d, part], y_id((1, 3)[d]))

    def y_relay(part):
        for d, back in ((0, 3), (1, 1)):
            source = lax.rem(y + back, 4)
            g_msg(d, part, source).wait_recv()
            start(y_msg(d, part, source))

    def y_wait(part):
        for d in (0, 1):
            y_msg(d, part, lax.rem(y + 2, 4)).wait_recv()

    def owned(x_dest, y_dest):
        return pl.ds(pl.multiple_of((y_dest * 4 + x_dest) * SUB, SUB), SUB)

    def r1_msg(d, part, cols):
        return remote(
            s1.at[part, d, :, cols], r1.at[part, d, :, cols],
            r1_send.at[part, d, cols.start // NQ], r1_recv.at[part, d, cols.start // NQ],
            x_id((1, 3)[d]),
        )

    def r2_msg(d, part, cols):
        return remote(
            s2.at[part, d, :, cols], r2.at[part, d, :, cols],
            r2_send.at[part, d, cols.start // NQ], r2_recv.at[part, d, cols.start // NQ],
            x_id((1, 3)[d]),
        )

    def stage1(part, cols):
        cpart[part, :, cols] = jnp.dot(
            a[pl.ds(part * 16 * SUB, 16 * SUB), :], w[:, cols], preferred_element_type=jnp.float32
        )
        far = lax.rem(x + 2, 4)
        for d in (0, 1):
            for i in (0, 1):
                s1[part, d, pl.ds(i * SUB, SUB), cols] = cpart[
                    part, owned(far, 2 * d + i), cols
                ].astype(jnp.bfloat16)
            start(r1_msg(d, part, cols))

    def stage2(part, cols):
        for d in (0, 1):
            near = lax.rem(x + (1, 3)[d], 4)
            r1_msg(d, part, cols).wait_recv()
            for y_dest in range(4):
                block = cpart[part, owned(near, y_dest), cols]
                if y_dest // 2 == d:
                    got = r1[part, d, pl.ds((y_dest - 2 * d) * SUB, SUB), cols]
                    block = block + got.astype(jnp.float32)
                s2[part, d, pl.ds(y_dest * SUB, SUB), cols] = block.astype(jnp.bfloat16)
            start(r2_msg(d, part, cols))

    def f_msg(part, cols, step, y_src, y_dest):
        column = pl.multiple_of(y_src * NBLK + cols.start, NQ)
        src = fb.at[part, aligned(y_dest, SUB), cols]
        dst = out_hbm.at[pl.ds(part * SUB, SUB), pl.ds(column, cols.size)]
        index = cols.start // NQ
        if step == 0:
            return pltpu.make_async_copy(src, dst, f_local.at[part, index])
        return remote(
            src, dst, f_send.at[part, index, step - 1], f_recv.at[part, index, step - 1], y_id(step)
        )

    def stage3(part, cols):
        for d in (0, 1):
            r2_msg(d, part, cols).wait_recv()
        for y_dest in range(4):
            rows = pl.ds(y_dest * SUB, SUB)
            summed = cpart[part, owned(x, y_dest), cols]
            for d in (0, 1):
                summed = summed + r2[part, d, rows, cols].astype(jnp.float32)
            fb[part, rows, cols] = summed.astype(jnp.bfloat16)
        for step in (1, 2, 3):
            start(f_msg(part, cols, step, y, lax.rem(y + step, 4)))
        f_msg(part, cols, 0, y, y).start()

    halo_send(1)
    w_send(D, 0, 1)
    w_send(D, 1, 1)
    for load in loads:
        load.wait()
    arrive(D, 0, 1)
    halo_send(2)
    arrive(D, 1, 1)
    attend_early()
    halo_send(3)
    w_send(U, 0, 1)
    w_send(U, 1, 1)
    arrive(D, 0, 2)
    arrive(D, 1, 2)
    halo_wait()
    for part in range(PARTS):
        attend_late(part)
        p_start(part)
    n01, n2, n3 = pl.ds(0, 1024), pl.ds(1024, 512), pl.ds(1536, 512)
    p_wait(0)
    g_start(0)
    arrive(U, 0, 1)
    arrive(D, 0, 3)
    p_wait(1)
    g_start(1)
    y_relay(0)
    arrive(U, 1, 1)
    arrive(D, 1, 3)
    p_wait(2)
    g_start(2)
    arrive(U, 0, 2)
    arrive(D, 0, 4)
    w_send(D, 2, 1)
    y_relay(1)
    arrive(U, 1, 2)
    w_send(U, 2, 1)
    arrive(D, 1, 4)
    w_send(D, 3, 1)
    arrive(U, 0, 3)
    y_relay(2)
    arrive(U, 1, 3)
    w_send(U, 3, 1)
    arrive(D, 2, 1)
    w_complete(0)
    w_complete(1)
    y_wait(0)
    stage1(0, n01)
    arrive(U, 2, 1)
    arrive(D, 3, 1)
    arrive(D, 2, 2)
    y_wait(1)
    stage1(1, n01)
    stage2(0, n01)
    arrive(U, 2, 2)
    arrive(U, 3, 1)
    arrive(D, 3, 2)
    y_wait(2)
    stage1(2, n01)
    stage2(1, n01)
    arrive(D, 2, 3)
    arrive(U, 3, 2)
    stage3(0, n01)
    arrive(U, 2, 3)
    arrive(D, 3, 3)
    stage2(2, n01)
    stage3(1, n01)
    arrive(D, 2, 4)
    w_complete(2)
    stage1(0, n2)
    stage3(2, n01)
    stage1(1, n2)
    stage2(0, n2)
    arrive(U, 3, 3)
    stage1(2, n2)
    stage2(1, n2)
    stage3(0, n2)
    arrive(D, 3, 4)
    w_complete(3)
    stage1(0, n3)
    stage2(2, n2)
    stage3(1, n2)
    stage1(1, n3)
    stage2(0, n3)
    stage3(2, n2)
    stage1(2, n3)
    stage2(1, n3)
    stage3(0, n3)
    stage2(2, n3)
    stage3(1, n3)
    stage3(2, n3)

    for cols in (n01, n2, n3):
        for part in range(PARTS):
            f_msg(part, cols, 0, y, y).wait()
            for step in (1, 2, 3):
                f_msg(part, cols, step, lax.rem(y + 4 - step, 4), y).wait_recv()
    for copy in sent:
        copy.wait_send()
    for part in range(PARTS):
        for jj in range(4):

            @pl.when(p_route(jj)[1] != z)
            def _():
                p_copy(part, jj).wait_send()


def on_device(queries, keys, values, doc_ids, block_mask, out_weight):
    any_space = pl.BlockSpec(memory_space=pl.ANY)
    dma = pltpu.SemaphoreType.DMA
    bf16, f32 = jnp.bfloat16, jnp.float32
    return pl.pallas_call(
        kernel,
        out_shape=jax.ShapeDtypeStruct((PIECE, 4 * NBLK), bf16),
        in_specs=[any_space] * 3
        + [pl.BlockSpec(memory_space=pltpu.VMEM), pl.BlockSpec(memory_space=pltpu.SMEM), any_space],
        out_specs=any_space,
        scratch_shapes=[
            pltpu.VMEM((ROWS, KBLK), bf16),
            pltpu.VMEM((WIN, KV), bf16),
            pltpu.VMEM((WIN, KV), bf16),
            pltpu.VMEM((ROWS, WIN), f32),
            pltpu.VMEM((2 * PARTS, 32 * SUB, HEAD_SIZE), f32),
            pltpu.VMEM((2 * PARTS, 32 * SUB, 2 * HEAD_SIZE), f32),
            pltpu.VMEM((KBLK, NBLK), bf16),
            pltpu.VMEM((4 * ROWS, KBLK), bf16),
            pltpu.VMEM((ROWS, KBLK), bf16),
            pltpu.VMEM((PARTS, 16 * SUB, NBLK), f32),
            pltpu.VMEM((PARTS, 2, 2 * SUB, NBLK), bf16),
            pltpu.VMEM((PARTS, 2, 4 * SUB, NBLK), bf16),
            pltpu.VMEM((PARTS, 2, 2 * SUB, NBLK), bf16),
            pltpu.VMEM((PARTS, 2, 4 * SUB, NBLK), bf16),
            pltpu.VMEM((PARTS, 4 * SUB, NBLK), bf16),
            dma((5,)),
            dma((3, 2)), dma((3, 2)),
            dma((CHUNKS, 4)), dma((CHUNKS, 4)),
            dma((CHUNKS, 3)), dma((CHUNKS, 3)),
            dma((CHUNKS, 7)), dma((CHUNKS, 7)),
            dma((PARTS, 4)), dma((PARTS, 4)),
            dma((2, PARTS)), dma((2, PARTS)),
            dma((2, PARTS)), dma((2, PARTS)),
            dma((PARTS, 2, CHUNKS)), dma((PARTS, 2, CHUNKS)),
            dma((PARTS, 2, CHUNKS)), dma((PARTS, 2, CHUNKS)),
            dma((PARTS, CHUNKS, 3)), dma((PARTS, CHUNKS, 3)), dma((PARTS, CHUNKS)),
        ],
        compiler_params=pltpu.CompilerParams(
            collective_id=0, has_side_effects=True, vmem_limit_bytes=60 * 1024 * 1024
        ),
    )(queries, keys, values, doc_ids.reshape(-1, 128), block_mask.T, out_weight)


def solution(mesh):
    in_specs = (
        P(("srv", "wsh"), "head"),
        P(("srv", "wsh"), "head"),
        P(("srv", "wsh"), "head"),
        P(),
        P(),
        P(("head", "wsh"), None),
    )
    out_specs = P(("srv", "head", "wsh"), None)
    return jax.shard_map(
        on_device, mesh=mesh, in_specs=in_specs, out_specs=out_specs, check_vma=False
    )
```

```python
from functools import partial
import math

import jax
import jax.numpy as jnp
from jax import lax
from jax.experimental import pallas as pl
from jax.experimental.pallas import tpu as pltpu
from jax.sharding import PartitionSpec as P

HEAD_SIZE = 128
SLAB_REACH = 4
MESH = pl.DeviceIdType.MESH

floor_score = -1e30
D, U = True, False

ROWS = 192
PIECE = 48
KV = 256
HEADS = 16
KBLK = 2048
NBLK = 2048
CUTS = (0, 512, 1024, 1536, 1792, NBLK)
CHUNKS = len(CUTS) - 1
WIN = SLAB_REACH * ROWS
PAIR = 2 * ROWS
PARTS = 3
SUB = PIECE // PARTS


def mod(a, n):
    return lax.rem(a + n, n)


def aligned(i, step):
    return pl.ds(pl.multiple_of(i * step, step), step)


def chunk(n):
    return pl.ds(CUTS[n], CUTS[n + 1] - CUTS[n])


def kernel(
    q_hbm, k_hbm, v_hbm, docs, mask, w_hbm, out_hbm,
    q, kw, vw, bias, peak, acc, w, a, abuf, cpart, s1, s2, r1, r2, fb,
    load_sem, h_send, h_recv, wm_send, wm_recv, wp_send, wp_recv, wc_send, wc_recv,
    p_send, p_recv, g_send, g_recv, y_send, y_recv, r1_send, r1_recv, r2_send, r2_recv,
    f_send, f_recv, f_local,
):
    srv = lax.axis_index("srv")
    x = lax.axis_index("head")
    z = lax.axis_index("wsh")
    y = lax.div(srv, 2)
    core = lax.rem(srv, 2)
    slab = srv * 8 + z
    ahead, behind = lax.rem(slab + 1, 64), lax.rem(slab + 63, 64)

    def slab_id(s):
        return {"srv": lax.div(s, 8), "wsh": lax.rem(s, 8)}

    def y_id(step):
        return {"srv": lax.rem(y + step, 4) * 2 + core}

    partner = {"srv": y * 2 + 1 - core}

    def x_id(step):
        return {"head": lax.rem(x + step, 4)}

    def z_id(step):
        return {"wsh": lax.rem(z + step, 8)}

    barrier = pltpu.get_barrier_semaphore()
    greeted = [slab_id(ahead), slab_id(behind), partner, x_id(1), x_id(3)]
    greeted += [y_id(step) for step in (1, 2, 3)] + [z_id(step) for step in range(1, 8)]
    for other in greeted:
        pl.semaphore_signal(barrier, inc=1, device_id=other, device_id_type=MESH)
    loads = [
        pltpu.make_async_copy(q_hbm, q, load_sem.at[0]),
        pltpu.make_async_copy(k_hbm, kw.at[pl.ds(0, ROWS)], load_sem.at[1]),
        pltpu.make_async_copy(v_hbm, vw.at[pl.ds(0, ROWS)], load_sem.at[2]),
    ]
    for part in (0, 1):
        loads.append(
            pltpu.make_async_copy(
                w_hbm.at[pl.ds(part * 128, 128), aligned(y, NBLK)],
                w.at[aligned(part * 8 + z, 128)], load_sem.at[3 + part],
            )
        )
    for load in loads:
        load.start()

    def docs_of(source):
        first = lax.div(source * 3, 2)
        row, after = docs[pl.ds(first, 1), :], docs[pl.ds(first + 1, 1), :]
        even = jnp.concatenate([row, after[:, :64]], axis=1)
        odd = jnp.concatenate([row[:, 64:], after], axis=1)
        return jnp.where(lax.rem(source, 2) == 0, even, odd).astype(jnp.float32)

    row_ids = lax.broadcasted_iota(jnp.int32, (ROWS, ROWS), 0)
    column_ids = lax.broadcasted_iota(jnp.int32, (ROWS, ROWS), 1)
    docs_query = jnp.sum(
        jnp.where(row_ids == column_ids, docs_of(slab), 0.0), axis=1, keepdims=True
    )
    for offset in range(SLAB_REACH):
        source = slab - offset
        live = (mask[offset, slab] > 0) & (source >= 0)
        seen = docs_query == docs_of(jnp.maximum(source, 0))
        if offset == 0:
            seen = seen & (column_ids <= row_ids)
        bias[:, pl.ds(offset * ROWS, ROWS)] = jnp.where(
            seen, jnp.where(live, 0.0, floor_score), floor_score
        )
    pl.semaphore_wait(barrier, len(greeted))

    sent = []

    def remote(src, dst, send_sem, recv_sem, device):
        return pltpu.make_async_remote_copy(
            src_ref=src, dst_ref=dst, send_sem=send_sem, recv_sem=recv_sem,
            device_id=device, device_id_type=MESH,
        )

    def halo(step, which):
        own = (k_hbm, v_hbm)[which]
        window = (kw, vw)[which]
        src = own if step == 1 else window.at[pl.ds((step - 1) * ROWS, ROWS)]
        return remote(
            src, window.at[pl.ds(step * ROWS, ROWS)],
            h_send.at[step - 1, which], h_recv.at[step - 1, which], slab_id(ahead),
        )

    def halo_send(step):
        for which in (0, 1):
            if step > 1:
                halo(step - 1, which).wait_recv()
            copy = halo(step, which)
            copy.start()
            sent.append(copy)

    def halo_wait():
        halo(3, 0).wait_recv()
        halo(3, 1).wait_recv()

    def w_piece(origin, n):
        return w.at[aligned(core * 8 + origin, 128), chunk(n)]

    def w_msg(down, n, step):
        sems = (wm_send, wm_recv) if down else (wp_send, wp_recv)
        origin = lax.rem(z + (step - 1 if down else 9 - step), 8)
        if step == 1:
            column = pl.multiple_of(y * NBLK + CUTS[n], 256)
            src = w_hbm.at[aligned(core, 128), pl.ds(column, chunk(n).size)]
        else:
            src = w_piece(origin, n)
        return remote(
            src, w_piece(origin, n), sems[0].at[n, step - 1], sems[1].at[n, step - 1],
            z_id(7 if down else 1),
        )

    def w_send(down, n, step):
        copy = w_msg(down, n, step)
        copy.start()
        sent.append(copy)

    def w_wait(down, n, step):
        origin = lax.rem(z + (step if down else 8 - step), 8)
        sems = (wm_send, wm_recv) if down else (wp_send, wp_recv)
        remote(
            w_piece(origin, n), w_piece(origin, n), sems[0].at[n, step - 1],
            sems[1].at[n, step - 1], z_id(7 if down else 1),
        ).wait_recv()

    def w_cross(down, n, step, half):
        origin = lax.rem(z + (step if down else 8 - step), 8)
        block = w.at[aligned(half * 8 + origin, 128), chunk(n)]
        index = step - 1 if down else step + 3
        return remote(block, block, wc_send.at[n, index], wc_recv.at[n, index], partner)

    def arrive(down, n, step):
        w_wait(down, n, step)
        if step < (4 if down else 3):
            w_send(down, n, step + 1)
        copy = w_cross(down, n, step, core)
        copy.start()
        sent.append(copy)

    def w_complete(n):
        for step in (1, 2, 3, 4):
            w_cross(True, n, step, 1 - core).wait_recv()
        for step in (1, 2, 3):
            w_cross(False, n, step, 1 - core).wait_recv()

    factor = math.log2(math.e) / math.sqrt(HEAD_SIZE)

    def attend(late, part, g):
        place = part * 2 + g
        columns = aligned(g, HEAD_SIZE)
        keys_seen = pl.ds(late * PAIR, PAIR)
        key, value = kw[keys_seen, columns], vw[keys_seen, columns]
        rows = [aligned(j * PARTS + part, SUB) for j in range(4)]
        stacked = jnp.concatenate(
            [q[rows[j], aligned(g * 8 + i, HEAD_SIZE)] for j in range(4) for i in range(8)], axis=0
        )
        scores = lax.dot_general(
            stacked, key, (((1,), (1,)), ((), ())), preferred_element_type=jnp.float32
        )
        scores = jnp.concatenate(
            [
                scores[j * 8 * SUB : (j + 1) * 8 * SUB].reshape(8, SUB, PAIR) * factor
                + bias[rows[j], keys_seen][None]
                for j in range(4)
            ],
            axis=0,
        ).reshape(32 * SUB, PAIR)
        largest = jnp.broadcast_to(jnp.max(scores, axis=-1, keepdims=True), (32 * SUB, HEAD_SIZE))
        if late:
            before = peak[place]
            largest = jnp.maximum(largest, before)
        terms = jnp.exp2(scores - jnp.concatenate([largest] * 3, axis=1)).astype(jnp.bfloat16)
        widened = jnp.concatenate([value, jnp.ones_like(value)], axis=1)
        both = jnp.dot(terms, widened, preferred_element_type=jnp.float32)
        if not late:
            peak[place] = largest
            acc[place] = both
            return
        rescale = jnp.exp2(before - largest)
        both = both + acc[place] * jnp.concatenate([rescale] * 2, axis=1)
        result = (both[:, :HEAD_SIZE] / both[:, HEAD_SIZE:]).astype(jnp.bfloat16)
        for j in range(4):
            for i in range(8):
                abuf[
                    aligned(part * 4 + j, SUB), aligned((i % 2) * 8 + g * 4 + i // 2, HEAD_SIZE)
                ] = result[(j * 8 + i) * SUB : (j * 8 + i + 1) * SUB]

    def attend_early():
        def step(i, carry):
            attend(0, lax.div(i, 2), lax.rem(i, 2))
            return carry

        lax.fori_loop(0, 2 * PARTS, step, 0)

    def attend_late(part):
        def step(g, carry):
            attend(1, part, g)
            return carry

        lax.fori_loop(0, 2, step, 0)

    def p_place(part, x_dest):
        return a.at[aligned((part * 4 + y) * 4 + x_dest, SUB)]

    def p_route(jj):
        j = lax.rem(jj + lax.div(z, 2), 4)
        return j, 4 * lax.rem(z, 2) + j

    def p_copy(part, jj):
        j, dest = p_route(jj)
        return remote(
            abuf.at[aligned(part * 4 + j, SUB)], p_place(part, lax.div(z, 2)),
            p_send.at[part, jj], p_recv.at[part, lax.div(z, 2)], {"wsh": dest},
        )

    def p_start(part):
        for jj in range(4):
            j, dest = p_route(jj)

            @pl.when(dest == z)
            def _():
                pltpu.make_async_copy(
                    abuf.at[aligned(part * 4 + j, SUB)], p_place(part, lax.div(z, 2)),
                    p_recv.at[part, lax.div(z, 2)],
                ).start()

            @pl.when(dest != z)
            def _():
                p_copy(part, jj).start()

    def p_wait(part):
        for x_dest in range(4):
            place = p_place(part, x_dest)
            pltpu.make_async_copy(place, place, p_recv.at[part, x_dest]).wait()

    def start(copy):
        copy.start()
        sent.append(copy)

    def g_msg(d, part, y_src):
        place = a.at[aligned(part * 4 + y_src, 4 * SUB)]
        return remote(place, place, g_send.at[d, part], g_recv.at[d, part], y_id((1, 3)[d]))

    def g_start(part):
        for d in (0, 1):
            start(g_msg(d, part, y))

    def y_msg(d, part, y_src):
        place = a.at[aligned((part * 4 + y_src) * 2 + d, 2 * SUB)]
        return remote(place, place, y_send.at[d, part], y_recv.at[d, part], y_id((1, 3)[d]))

    def y_relay(part):
        for d, back in ((0, 3), (1, 1)):
            source = lax.rem(y + back, 4)
            g_msg(d, part, source).wait_recv()
            start(y_msg(d, part, source))

    def y_wait(part):
        for d in (0, 1):
            y_msg(d, part, lax.rem(y + 2, 4)).wait_recv()

    def owned(x_dest, y_dest):
        return pl.ds(pl.multiple_of((y_dest * 4 + x_dest) * SUB, SUB), SUB)

    def r1_msg(d, part, n):
        cols = chunk(n)
        return remote(
            s1.at[part, d, :, cols], r1.at[part, d, :, cols],
            r1_send.at[part, d, n], r1_recv.at[part, d, n],
            x_id((1, 3)[d]),
        )

    def r2_msg(d, part, n):
        cols = chunk(n)
        return remote(
            s2.at[part, d, :, cols], r2.at[part, d, :, cols],
            r2_send.at[part, d, n], r2_recv.at[part, d, n],
            x_id((1, 3)[d]),
        )

    def stage1(part, n):
        cols = chunk(n)
        cpart[part, :, cols] = jnp.dot(
            a[pl.ds(part * 16 * SUB, 16 * SUB), :], w[:, cols], preferred_element_type=jnp.float32
        )
        far = lax.rem(x + 2, 4)
        for d in (0, 1):
            for i in (0, 1):
                s1[part, d, pl.ds(i * SUB, SUB), cols] = cpart[
                    part, owned(far, 2 * d + i), cols
                ].astype(jnp.bfloat16)
            start(r1_msg(d, part, n))

    def stage2(part, n):
        cols = chunk(n)
        for d in (0, 1):
            near = lax.rem(x + (1, 3)[d], 4)
            r1_msg(d, part, n).wait_recv()
            for y_dest in range(4):
                block = cpart[part, owned(near, y_dest), cols]
                if y_dest // 2 == d:
                    got = r1[part, d, pl.ds((y_dest - 2 * d) * SUB, SUB), cols]
                    block = block + got.astype(jnp.float32)
                s2[part, d, pl.ds(y_dest * SUB, SUB), cols] = block.astype(jnp.bfloat16)
            start(r2_msg(d, part, n))

    def f_msg(part, n, step, y_src, y_dest):
        cols = chunk(n)
        column = pl.multiple_of(y_src * NBLK + CUTS[n], 256)
        src = fb.at[part, aligned(y_dest, SUB), cols]
        dst = out_hbm.at[pl.ds(part * SUB, SUB), pl.ds(column, cols.size)]
        if step == 0:
            return pltpu.make_async_copy(src, dst, f_local.at[part, n])
        return remote(
            src, dst, f_send.at[part, n, step - 1], f_recv.at[part, n, step - 1], y_id(step)
        )

    def stage3(part, n):
        cols = chunk(n)
        for d in (0, 1):
            r2_msg(d, part, n).wait_recv()
        for y_dest in range(4):
            rows = pl.ds(y_dest * SUB, SUB)
            summed = cpart[part, owned(x, y_dest), cols]
            for d in (0, 1):
                summed = summed + r2[part, d, rows, cols].astype(jnp.float32)
            fb[part, rows, cols] = summed.astype(jnp.bfloat16)
        for step in (1, 2, 3):
            start(f_msg(part, n, step, y, lax.rem(y + step, 4)))
        f_msg(part, n, 0, y, y).start()

    halo_send(1)
    w_send(D, 0, 1)
    w_send(U, 4, 1)
    w_send(D, 1, 1)
    for load in loads:
        load.wait()
    w_send(D, 4, 1)
    halo_send(2)
    arrive(D, 0, 1)
    arrive(D, 1, 1)
    w_send(U, 0, 1)
    halo_send(3)
    w_send(D, 2, 1)
    attend_early()
    arrive(D, 1, 2)
    w_send(D, 3, 1)
    w_send(U, 1, 1)
    halo_wait()
    attend_late(0)
    p_start(0)
    attend_late(1)
    p_start(1)
    attend_late(2)
    p_start(2)
    arrive(D, 4, 1)
    arrive(D, 0, 2)
    arrive(D, 3, 1)
    arrive(U, 1, 1)
    arrive(D, 1, 3)
    p_wait(0)
    g_start(0)
    p_wait(1)
    g_start(1)
    arrive(D, 4, 2)
    y_relay(0)
    arrive(U, 0, 1)
    p_wait(2)
    g_start(2)
    arrive(D, 0, 3)
    arrive(U, 1, 2)
    arrive(U, 0, 2)
    y_relay(1)
    arrive(U, 1, 3)
    w_send(U, 2, 1)
    arrive(D, 2, 1)
    arrive(D, 1, 4)
    w_send(U, 3, 1)
    w_complete(1)
    y_relay(2)
    arrive(D, 3, 2)
    y_wait(0)
    arrive(D, 0, 4)
    arrive(U, 4, 1)
    arrive(D, 4, 3)
    stage1(0, 1)
    arrive(U, 0, 3)
    arrive(U, 2, 1)
    arrive(D, 2, 2)
    y_wait(1)
    stage1(1, 1)
    w_complete(0)
    stage2(0, 1)
    arrive(U, 3, 1)
    stage1(0, 0)
    stage1(1, 0)
    arrive(U, 4, 2)
    arrive(U, 2, 2)
    y_wait(2)
    stage2(1, 1)
    arrive(D, 2, 3)
    stage1(2, 1)
    stage1(2, 0)
    arrive(D, 4, 4)
    arrive(U, 4, 3)
    stage2(1, 0)
    stage2(0, 0)
    arrive(U, 3, 2)
    arrive(D, 3, 3)
    w_complete(4)
    stage1(2, 4)
    arrive(U, 2, 3)
    stage2(2, 0)
    arrive(D, 2, 4)
    stage2(2, 1)
    stage1(1, 4)
    arrive(U, 3, 3)
    stage3(1, 0)
    w_complete(2)
    arrive(D, 3, 4)
    stage1(1, 2)
    stage2(2, 4)
    stage1(0, 4)
    w_complete(3)
    stage1(1, 3)
    stage1(0, 2)
    stage2(1, 2)
    stage1(2, 2)
    stage1(0, 3)
    stage2(0, 2)
    stage2(0, 4)
    stage3(0, 1)
    stage3(1, 1)
    stage3(2, 1)
    stage2(1, 4)
    stage1(2, 3)
    stage2(0, 3)
    stage3(1, 2)
    stage3(0, 2)
    stage2(2, 2)
    stage2(1, 3)
    stage3(2, 4)
    stage3(1, 4)
    stage3(2, 0)
    stage3(0, 0)
    stage2(2, 3)
    stage3(0, 4)
    stage3(0, 3)
    stage3(2, 2)
    stage3(1, 3)
    stage3(2, 3)

    for n in range(CHUNKS):
        for part in range(PARTS):
            f_msg(part, n, 0, y, y).wait()
            for step in (1, 2, 3):
                f_msg(part, n, step, lax.rem(y + 4 - step, 4), y).wait_recv()
    for copy in sent:
        copy.wait_send()
    for part in range(PARTS):
        for jj in range(4):

            @pl.when(p_route(jj)[1] != z)
            def _():
                p_copy(part, jj).wait_send()


def on_device(queries, keys, values, doc_ids, block_mask, out_weight):
    any_space = pl.BlockSpec(memory_space=pl.ANY)
    dma = pltpu.SemaphoreType.DMA
    bf16, f32 = jnp.bfloat16, jnp.float32
    return pl.pallas_call(
        kernel,
        out_shape=jax.ShapeDtypeStruct((PIECE, 4 * NBLK), bf16),
        in_specs=[any_space] * 3
        + [pl.BlockSpec(memory_space=pltpu.VMEM), pl.BlockSpec(memory_space=pltpu.SMEM), any_space],
        out_specs=any_space,
        scratch_shapes=[
            pltpu.VMEM((ROWS, KBLK), bf16),
            pltpu.VMEM((WIN, KV), bf16),
            pltpu.VMEM((WIN, KV), bf16),
            pltpu.VMEM((ROWS, WIN), f32),
            pltpu.VMEM((2 * PARTS, 32 * SUB, HEAD_SIZE), f32),
            pltpu.VMEM((2 * PARTS, 32 * SUB, 2 * HEAD_SIZE), f32),
            pltpu.VMEM((KBLK, NBLK), bf16),
            pltpu.VMEM((4 * ROWS, KBLK), bf16),
            pltpu.VMEM((ROWS, KBLK), bf16),
            pltpu.VMEM((PARTS, 16 * SUB, NBLK), f32),
            pltpu.VMEM((PARTS, 2, 2 * SUB, NBLK), bf16),
            pltpu.VMEM((PARTS, 2, 4 * SUB, NBLK), bf16),
            pltpu.VMEM((PARTS, 2, 2 * SUB, NBLK), bf16),
            pltpu.VMEM((PARTS, 2, 4 * SUB, NBLK), bf16),
            pltpu.VMEM((PARTS, 4 * SUB, NBLK), bf16),
            dma((5,)),
            dma((3, 2)), dma((3, 2)),
            dma((CHUNKS, 4)), dma((CHUNKS, 4)),
            dma((CHUNKS, 3)), dma((CHUNKS, 3)),
            dma((CHUNKS, 7)), dma((CHUNKS, 7)),
            dma((PARTS, 4)), dma((PARTS, 4)),
            dma((2, PARTS)), dma((2, PARTS)),
            dma((2, PARTS)), dma((2, PARTS)),
            dma((PARTS, 2, CHUNKS)), dma((PARTS, 2, CHUNKS)),
            dma((PARTS, 2, CHUNKS)), dma((PARTS, 2, CHUNKS)),
            dma((PARTS, CHUNKS, 3)), dma((PARTS, CHUNKS, 3)), dma((PARTS, CHUNKS)),
        ],
        compiler_params=pltpu.CompilerParams(
            collective_id=0, has_side_effects=True, vmem_limit_bytes=60 * 1024 * 1024
        ),
    )(queries, keys, values, doc_ids.reshape(-1, 128), block_mask.T, out_weight)


def solution(mesh):
    in_specs = (
        P(("srv", "wsh"), "head"),
        P(("srv", "wsh"), "head"),
        P(("srv", "wsh"), "head"),
        P(),
        P(),
        P(("head", "wsh"), None),
    )
    out_specs = P(("srv", "head", "wsh"), None)
    return jax.shard_map(
        on_device, mesh=mesh, in_specs=in_specs, out_specs=out_specs, check_vma=False
    )
```

```python
from functools import partial
import math

import jax
import jax.numpy as jnp
from jax import lax
from jax.experimental import pallas as pl
from jax.experimental.pallas import tpu as pltpu
from jax.sharding import PartitionSpec as P

HEAD_SIZE = 128
SLAB_REACH = 4
MESH = pl.DeviceIdType.MESH

floor_score = -1e30
D, U = True, False

ROWS = 192
PIECE = 48
KV = 256
HEADS = 16
KBLK = 2048
NBLK = 2048
CUTS = (0, 512, 1024, 1536, 1792, NBLK)
CHUNKS = len(CUTS) - 1
WIN = SLAB_REACH * ROWS
PAIR = 2 * ROWS
PARTS = 3
SUB = PIECE // PARTS


def mod(a, n):
    return lax.rem(a + n, n)


def aligned(i, step):
    return pl.ds(pl.multiple_of(i * step, step), step)


def chunk(n):
    return pl.ds(CUTS[n], CUTS[n + 1] - CUTS[n])


def kernel(
    q_hbm, k_hbm, v_hbm, docs, mask, w_hbm, out_hbm,
    q, kw, vw, bias, peak, acc, w, a, abuf, cpart, s1, s2, r1, r2, fb,
    load_sem, h_send, h_recv, wm_send, wm_recv, wp_send, wp_recv, wc_send, wc_recv,
    p_send, p_recv, g_send, g_recv, y_send, y_recv, r1_send, r1_recv, r2_send, r2_recv,
    f_send, f_recv, f_local,
):
    srv = lax.axis_index("srv")
    x = lax.axis_index("head")
    z = lax.axis_index("wsh")
    y = lax.div(srv, 2)
    core = lax.rem(srv, 2)
    slab = srv * 8 + z
    ahead, behind = lax.rem(slab + 1, 64), lax.rem(slab + 63, 64)

    def slab_id(s):
        return {"srv": lax.div(s, 8), "wsh": lax.rem(s, 8)}

    def y_id(step):
        return {"srv": lax.rem(y + step, 4) * 2 + core}

    partner = {"srv": y * 2 + 1 - core}

    def x_id(step):
        return {"head": lax.rem(x + step, 4)}

    def z_id(step):
        return {"wsh": lax.rem(z + step, 8)}

    barrier = pltpu.get_barrier_semaphore()
    greeted = [slab_id(ahead), slab_id(behind), partner, x_id(1), x_id(3)]
    greeted += [y_id(step) for step in (1, 2, 3)] + [z_id(step) for step in range(1, 8)]
    for other in greeted:
        pl.semaphore_signal(barrier, inc=1, device_id=other, device_id_type=MESH)
    loads = [
        pltpu.make_async_copy(q_hbm, q, load_sem.at[0]),
        pltpu.make_async_copy(k_hbm, kw.at[pl.ds(0, ROWS)], load_sem.at[1]),
        pltpu.make_async_copy(v_hbm, vw.at[pl.ds(0, ROWS)], load_sem.at[2]),
    ]
    for part in (0, 1):
        loads.append(
            pltpu.make_async_copy(
                w_hbm.at[pl.ds(part * 128, 128), aligned(y, NBLK)],
                w.at[aligned(part * 8 + z, 128)], load_sem.at[3 + part],
            )
        )
    for load in loads:
        load.start()

    def docs_of(source):
        first = lax.div(source * 3, 2)
        row, after = docs[pl.ds(first, 1), :], docs[pl.ds(first + 1, 1), :]
        even = jnp.concatenate([row, after[:, :64]], axis=1)
        odd = jnp.concatenate([row[:, 64:], after], axis=1)
        return jnp.where(lax.rem(source, 2) == 0, even, odd).astype(jnp.float32)

    row_ids = lax.broadcasted_iota(jnp.int32, (ROWS, ROWS), 0)
    column_ids = lax.broadcasted_iota(jnp.int32, (ROWS, ROWS), 1)
    docs_query = jnp.sum(
        jnp.where(row_ids == column_ids, docs_of(slab), 0.0), axis=1, keepdims=True
    )
    for offset in range(SLAB_REACH):
        source = slab - offset
        live = (mask[offset, slab] > 0) & (source >= 0)
        seen = docs_query == docs_of(jnp.maximum(source, 0))
        if offset == 0:
            seen = seen & (column_ids <= row_ids)
        bias[:, pl.ds(offset * ROWS, ROWS)] = jnp.where(
            seen, jnp.where(live, 0.0, floor_score), floor_score
        )
    pl.semaphore_wait(barrier, len(greeted))

    sent = []

    def remote(src, dst, send_sem, recv_sem, device):
        return pltpu.make_async_remote_copy(
            src_ref=src, dst_ref=dst, send_sem=send_sem, recv_sem=recv_sem,
            device_id=device, device_id_type=MESH,
        )

    def halo(step, which):
        own = (k_hbm, v_hbm)[which]
        window = (kw, vw)[which]
        src = own if step == 1 else window.at[pl.ds((step - 1) * ROWS, ROWS)]
        return remote(
            src, window.at[pl.ds(step * ROWS, ROWS)],
            h_send.at[step - 1, which], h_recv.at[step - 1, which], slab_id(ahead),
        )

    def halo_send(step):
        for which in (0, 1):
            if step > 1:
                halo(step - 1, which).wait_recv()
            copy = halo(step, which)
            copy.start()
            sent.append(copy)

    def halo_wait():
        halo(3, 0).wait_recv()
        halo(3, 1).wait_recv()

    def w_piece(origin, n):
        return w.at[aligned(core * 8 + origin, 128), chunk(n)]

    def w_msg(down, n, step):
        sems = (wm_send, wm_recv) if down else (wp_send, wp_recv)
        origin = lax.rem(z + (step - 1 if down else 9 - step), 8)
        if step == 1:
            column = pl.multiple_of(y * NBLK + CUTS[n], 256)
            src = w_hbm.at[aligned(core, 128), pl.ds(column, chunk(n).size)]
        else:
            src = w_piece(origin, n)
        return remote(
            src, w_piece(origin, n), sems[0].at[n, step - 1], sems[1].at[n, step - 1],
            z_id(7 if down else 1),
        )

    def w_send(down, n, step):
        copy = w_msg(down, n, step)
        copy.start()
        sent.append(copy)

    def w_wait(down, n, step):
        origin = lax.rem(z + (step if down else 8 - step), 8)
        sems = (wm_send, wm_recv) if down else (wp_send, wp_recv)
        remote(
            w_piece(origin, n), w_piece(origin, n), sems[0].at[n, step - 1],
            sems[1].at[n, step - 1], z_id(7 if down else 1),
        ).wait_recv()

    def w_cross(down, n, step, half):
        origin = lax.rem(z + (step if down else 8 - step), 8)
        block = w.at[aligned(half * 8 + origin, 128), chunk(n)]
        index = step - 1 if down else step + 3
        return remote(block, block, wc_send.at[n, index], wc_recv.at[n, index], partner)

    def arrive(down, n, step):
        w_wait(down, n, step)
        if step < (4 if down else 3):
            w_send(down, n, step + 1)
        copy = w_cross(down, n, step, core)
        copy.start()
        sent.append(copy)

    def w_complete(n):
        for step in (1, 2, 3, 4):
            w_cross(True, n, step, 1 - core).wait_recv()
        for step in (1, 2, 3):
            w_cross(False, n, step, 1 - core).wait_recv()

    factor = math.log2(math.e) / math.sqrt(HEAD_SIZE)

    def attend(late, part, g):
        place = part * 2 + g
        columns = aligned(g, HEAD_SIZE)
        keys_seen = pl.ds(late * PAIR, PAIR)
        key, value = kw[keys_seen, columns], vw[keys_seen, columns]
        rows = [aligned(j * PARTS + part, SUB) for j in range(4)]
        stacked = jnp.concatenate(
            [q[rows[j], aligned(g * 8 + i, HEAD_SIZE)] for j in range(4) for i in range(8)], axis=0
        )
        scores = lax.dot_general(
            stacked, key, (((1,), (1,)), ((), ())), preferred_element_type=jnp.float32
        )
        scores = jnp.concatenate(
            [
                scores[j * 8 * SUB : (j + 1) * 8 * SUB].reshape(8, SUB, PAIR) * factor
                + bias[rows[j], keys_seen][None]
                for j in range(4)
            ],
            axis=0,
        ).reshape(32 * SUB, PAIR)
        largest = jnp.broadcast_to(jnp.max(scores, axis=-1, keepdims=True), (32 * SUB, HEAD_SIZE))
        if late:
            before = peak[place]
            largest = jnp.maximum(largest, before)
        terms = jnp.exp2(scores - jnp.concatenate([largest] * 3, axis=1)).astype(jnp.bfloat16)
        widened = jnp.concatenate([value, jnp.ones_like(value)], axis=1)
        both = jnp.dot(terms, widened, preferred_element_type=jnp.float32)
        if not late:
            peak[place] = largest
            acc[place] = both
            return
        rescale = jnp.exp2(before - largest)
        both = both + acc[place] * jnp.concatenate([rescale] * 2, axis=1)
        result = (both[:, :HEAD_SIZE] / both[:, HEAD_SIZE:]).astype(jnp.bfloat16)
        for j in range(4):
            for i in range(8):
                abuf[
                    aligned(part * 4 + j, SUB), aligned((i % 2) * 8 + g * 4 + i // 2, HEAD_SIZE)
                ] = result[(j * 8 + i) * SUB : (j * 8 + i + 1) * SUB]

    def attend_early():
        def step(i, carry):
            attend(0, lax.div(i, 2), lax.rem(i, 2))
            return carry

        lax.fori_loop(0, 2 * PARTS, step, 0)

    def attend_late(part):
        def step(g, carry):
            attend(1, part, g)
            return carry

        lax.fori_loop(0, 2, step, 0)

    def p_place(part, x_dest):
        return a.at[aligned((part * 4 + y) * 4 + x_dest, SUB)]

    def p_route(jj):
        j = lax.rem(jj + lax.div(z, 2), 4)
        return j, 4 * lax.rem(z, 2) + j

    def p_copy(part, jj):
        j, dest = p_route(jj)
        return remote(
            abuf.at[aligned(part * 4 + j, SUB)], p_place(part, lax.div(z, 2)),
            p_send.at[part, jj], p_recv.at[part, lax.div(z, 2)], {"wsh": dest},
        )

    def p_start(part):
        for jj in range(4):
            j, dest = p_route(jj)

            @pl.when(dest == z)
            def _():
                pltpu.make_async_copy(
                    abuf.at[aligned(part * 4 + j, SUB)], p_place(part, lax.div(z, 2)),
                    p_recv.at[part, lax.div(z, 2)],
                ).start()

            @pl.when(dest != z)
            def _():
                p_copy(part, jj).start()

    def p_wait(part):
        for x_dest in range(4):
            place = p_place(part, x_dest)
            pltpu.make_async_copy(place, place, p_recv.at[part, x_dest]).wait()

    def start(copy):
        copy.start()
        sent.append(copy)

    def g_msg(d, part, y_src):
        place = a.at[aligned(part * 4 + y_src, 4 * SUB)]
        return remote(place, place, g_send.at[d, part], g_recv.at[d, part], y_id((1, 3)[d]))

    def g_start(part):
        for d in (0, 1):
            start(g_msg(d, part, y))

    def y_msg(d, part, y_src):
        place = a.at[aligned((part * 4 + y_src) * 2 + d, 2 * SUB)]
        return remote(place, place, y_send.at[d, part], y_recv.at[d, part], y_id((1, 3)[d]))

    def y_relay(part):
        for d, back in ((0, 3), (1, 1)):
            source = lax.rem(y + back, 4)
            g_msg(d, part, source).wait_recv()
            start(y_msg(d, part, source))

    def y_wait(part):
        for d in (0, 1):
            y_msg(d, part, lax.rem(y + 2, 4)).wait_recv()

    def owned(x_dest, y_dest):
        return pl.ds(pl.multiple_of((y_dest * 4 + x_dest) * SUB, SUB), SUB)

    def r1_msg(d, part, n):
        cols = chunk(n)
        return remote(
            s1.at[part, d, :, cols], r1.at[part, d, :, cols],
            r1_send.at[part, d, n], r1_recv.at[part, d, n],
            x_id((1, 3)[d]),
        )

    def r2_msg(d, part, n):
        cols = chunk(n)
        return remote(
            s2.at[part, d, :, cols], r2.at[part, d, :, cols],
            r2_send.at[part, d, n], r2_recv.at[part, d, n],
            x_id((1, 3)[d]),
        )

    def stage1(part, n):
        cols = chunk(n)
        cpart[part, :, cols] = jnp.dot(
            a[pl.ds(part * 16 * SUB, 16 * SUB), :], w[:, cols], preferred_element_type=jnp.float32
        )
        far = lax.rem(x + 2, 4)
        for d in (0, 1):
            for i in (0, 1):
                s1[part, d, pl.ds(i * SUB, SUB), cols] = cpart[
                    part, owned(far, 2 * d + i), cols
                ].astype(jnp.bfloat16)
            start(r1_msg(d, part, n))

    def stage2(part, n):
        cols = chunk(n)
        for d in (0, 1):
            near = lax.rem(x + (1, 3)[d], 4)
            r1_msg(d, part, n).wait_recv()
            for y_dest in range(4):
                block = cpart[part, owned(near, y_dest), cols]
                if y_dest // 2 == d:
                    got = r1[part, d, pl.ds((y_dest - 2 * d) * SUB, SUB), cols]
                    block = block + got.astype(jnp.float32)
                s2[part, d, pl.ds(y_dest * SUB, SUB), cols] = block.astype(jnp.bfloat16)
            start(r2_msg(d, part, n))

    def f_msg(part, n, step, y_src, y_dest):
        cols = chunk(n)
        column = pl.multiple_of(y_src * NBLK + CUTS[n], 256)
        src = fb.at[part, aligned(y_dest, SUB), cols]
        dst = out_hbm.at[pl.ds(part * SUB, SUB), pl.ds(column, cols.size)]
        if step == 0:
            return pltpu.make_async_copy(src, dst, f_local.at[part, n])
        return remote(
            src, dst, f_send.at[part, n, step - 1], f_recv.at[part, n, step - 1], y_id(step)
        )

    def stage3(part, n):
        cols = chunk(n)
        for d in (0, 1):
            r2_msg(d, part, n).wait_recv()
        for y_dest in range(4):
            rows = pl.ds(y_dest * SUB, SUB)
            summed = cpart[part, owned(x, y_dest), cols]
            for d in (0, 1):
                summed = summed + r2[part, d, rows, cols].astype(jnp.float32)
            fb[part, rows, cols] = summed.astype(jnp.bfloat16)
        for step in (1, 2, 3):
            start(f_msg(part, n, step, y, lax.rem(y + step, 4)))
        f_msg(part, n, 0, y, y).start()

    halo_send(1)
    w_send(D, 0, 1)
    w_send(U, 4, 1)
    w_send(D, 1, 1)
    for load in loads:
        load.wait()
    w_send(D, 4, 1)
    halo_send(2)
    arrive(D, 0, 1)
    arrive(D, 1, 1)
    w_send(U, 0, 1)
    halo_send(3)
    w_send(D, 2, 1)
    attend_early()
    arrive(D, 1, 2)
    w_send(D, 3, 1)
    w_send(U, 1, 1)
    halo_wait()
    attend_late(0)
    p_start(0)
    attend_late(1)
    p_start(1)
    attend_late(2)
    p_start(2)
    arrive(D, 4, 1)
    arrive(D, 0, 2)
    arrive(D, 3, 1)
    arrive(U, 1, 1)
    arrive(D, 1, 3)
    p_wait(0)
    g_start(0)
    p_wait(1)
    g_start(1)
    arrive(D, 4, 2)
    y_relay(0)
    arrive(U, 0, 1)
    p_wait(2)
    g_start(2)
    arrive(D, 0, 3)
    arrive(U, 1, 2)
    arrive(U, 0, 2)
    y_relay(1)
    arrive(U, 1, 3)
    w_send(U, 2, 1)
    arrive(D, 2, 1)
    arrive(D, 1, 4)
    w_send(U, 3, 1)
    w_complete(1)
    y_relay(2)
    arrive(D, 3, 2)
    y_wait(0)
    arrive(D, 0, 4)
    arrive(U, 4, 1)
    arrive(D, 4, 3)
    stage1(0, 1)
    arrive(U, 0, 3)
    arrive(U, 2, 1)
    arrive(D, 2, 2)
    y_wait(1)
    stage1(1, 1)
    w_complete(0)
    stage2(0, 1)
    arrive(U, 3, 1)
    stage1(0, 0)
    stage1(1, 0)
    arrive(U, 4, 2)
    arrive(U, 2, 2)
    y_wait(2)
    stage2(1, 1)
    arrive(D, 2, 3)
    stage1(2, 1)
    stage1(2, 0)
    arrive(D, 4, 4)
    arrive(U, 4, 3)
    stage2(1, 0)
    stage2(0, 0)
    arrive(U, 3, 2)
    arrive(D, 3, 3)
    w_complete(4)
    stage1(2, 4)
    arrive(U, 2, 3)
    stage2(2, 0)
    arrive(D, 2, 4)
    stage2(2, 1)
    stage1(1, 4)
    arrive(U, 3, 3)
    stage3(1, 0)
    w_complete(2)
    arrive(D, 3, 4)
    stage1(1, 2)
    stage2(2, 4)
    stage1(0, 4)
    w_complete(3)
    stage1(1, 3)
    stage1(0, 2)
    stage2(1, 2)
    stage1(2, 2)
    stage1(0, 3)
    stage2(0, 2)
    stage2(0, 4)
    stage3(0, 1)
    stage3(1, 1)
    stage3(2, 1)
    stage2(1, 4)
    stage1(2, 3)
    stage2(0, 3)
    stage3(1, 2)
    stage3(0, 2)
    stage2(2, 2)
    stage2(1, 3)
    stage3(2, 4)
    stage3(1, 4)
    stage3(2, 0)
    stage3(0, 0)
    stage2(2, 3)
    stage3(0, 4)
    stage3(0, 3)
    stage3(2, 2)
    stage3(1, 3)
    stage3(2, 3)

    for n in range(CHUNKS):
        for part in range(PARTS):
            f_msg(part, n, 0, y, y).wait()
            for step in (1, 2, 3):
                f_msg(part, n, step, lax.rem(y + 4 - step, 4), y).wait_recv()
    for copy in sent:
        copy.wait_send()
    for part in range(PARTS):
        for jj in range(4):

            @pl.when(p_route(jj)[1] != z)
            def _():
                p_copy(part, jj).wait_send()


def on_device(queries, keys, values, doc_ids, block_mask, out_weight):
    any_space = pl.BlockSpec(memory_space=pl.ANY)
    dma = pltpu.SemaphoreType.DMA
    bf16, f32 = jnp.bfloat16, jnp.float32
    return pl.pallas_call(
        kernel,
        out_shape=pltpu.VMEM((PIECE, 4 * NBLK), bf16),
        in_specs=[any_space] * 3
        + [pl.BlockSpec(memory_space=pltpu.VMEM), pl.BlockSpec(memory_space=pltpu.SMEM), any_space],
        out_specs=pl.BlockSpec(memory_space=pltpu.VMEM),
        scratch_shapes=[
            pltpu.VMEM((ROWS, KBLK), bf16),
            pltpu.VMEM((WIN, KV), bf16),
            pltpu.VMEM((WIN, KV), bf16),
            pltpu.VMEM((ROWS, WIN), f32),
            pltpu.VMEM((2 * PARTS, 32 * SUB, HEAD_SIZE), f32),
            pltpu.VMEM((2 * PARTS, 32 * SUB, 2 * HEAD_SIZE), f32),
            pltpu.VMEM((KBLK, NBLK), bf16),
            pltpu.VMEM((4 * ROWS, KBLK), bf16),
            pltpu.VMEM((ROWS, KBLK), bf16),
            pltpu.VMEM((PARTS, 16 * SUB, NBLK), f32),
            pltpu.VMEM((PARTS, 2, 2 * SUB, NBLK), bf16),
            pltpu.VMEM((PARTS, 2, 4 * SUB, NBLK), bf16),
            pltpu.VMEM((PARTS, 2, 2 * SUB, NBLK), bf16),
            pltpu.VMEM((PARTS, 2, 4 * SUB, NBLK), bf16),
            pltpu.VMEM((PARTS, 4 * SUB, NBLK), bf16),
            dma((5,)),
            dma((3, 2)), dma((3, 2)),
            dma((CHUNKS, 4)), dma((CHUNKS, 4)),
            dma((CHUNKS, 3)), dma((CHUNKS, 3)),
            dma((CHUNKS, 7)), dma((CHUNKS, 7)),
            dma((PARTS, 4)), dma((PARTS, 4)),
            dma((2, PARTS)), dma((2, PARTS)),
            dma((2, PARTS)), dma((2, PARTS)),
            dma((PARTS, 2, CHUNKS)), dma((PARTS, 2, CHUNKS)),
            dma((PARTS, 2, CHUNKS)), dma((PARTS, 2, CHUNKS)),
            dma((PARTS, CHUNKS, 3)), dma((PARTS, CHUNKS, 3)), dma((PARTS, CHUNKS)),
        ],
        compiler_params=pltpu.CompilerParams(
            collective_id=0, has_side_effects=True, vmem_limit_bytes=60 * 1024 * 1024
        ),
    )(queries, keys, values, doc_ids.reshape(-1, 128), block_mask.T, out_weight)


def solution(mesh):
    in_specs = (
        P(("srv", "wsh"), "head"),
        P(("srv", "wsh"), "head"),
        P(("srv", "wsh"), "head"),
        P(),
        P(),
        P(("head", "wsh"), None),
    )
    out_specs = P(("srv", "head", "wsh"), None)
    return jax.shard_map(
        on_device, mesh=mesh, in_specs=in_specs, out_specs=out_specs, check_vma=False
    )
```
